128 devices in a mesh: dp: 8 (over z, core), ctx: 16 (over x, y).
Axes of the slice: x: 4, y: 4, z: 4, core: 2. Of those that a mesh axis runs over, the one named last changes fastest.
Arguments:
- tokens: bfloat16 [32768, 2048], P(('dp', 'ctx')), parts along dimension 0, may hold values from -80 to 80
- qkv_weight: bfloat16 [2048, 3072], P('ctx'), may hold values from -0.125 to 0.125
- out_weight: bfloat16 [1024, 2048], P('ctx'), may hold values from -0.1875 to 0.1875
- prior_state: float32 [64, 128, 128], P('dp'), parts along dimension 0, may hold values from -240 to 240
- expert_ids: int32 [32768, 4], P(('dp', 'ctx')), parts along dimension 0, may hold values from 0 to 15, all different within a row; in each aligned block of 256 rows (0 to 255, 256 to 511, ...) at most 96 rows name the same one
- gate_weights: float32 [32768, 4], P(('dp', 'ctx')), parts along dimension 0, may hold values from 0.1 to 1
- expert_in: bfloat16 [16, 2048, 2048], P('ctx'), may hold values from -0.125 to 0.125
- expert_out: bfloat16 [16, 1024, 2048], P('ctx'), may hold values from -0.1875 to 0.1875
Outputs:
- layer_out: bfloat16 [32768, 2048], P(('dp', 'ctx')), parts along dimension 0
The draws below stay inside these ranges and needn't reach their ends.
There are 8 independent parts, one for each index of `dp`. The reference program is written for one: setup_inputs(seed, part) draws one part's arguments, and reference() takes and returns one part's arrays. A program takes and returns all parts, laid end to end along the dimension named above; an argument that names none is the same for every part. Nothing has to cross between parts.
Inputs may be any that keep to these rules, and one draw needn't show every extreme that they name: `expert_ids`: within the 256 rows of one device no expert is named more than 96 times, and in some device's rows some expert is named exactly 96 times.
All inputs are finite; a program needn't handle non-finite values.
Results may differ from the reference program's by a relative error of at most 0.006.
Values may be sent and summed in bfloat16 or wider, within the bound.
No kernel may reach another device: no remote copies, remote signals or barrier semaphores. Data moves between devices by JAX's collectives and lax.ppermute only.
A program may use at most 128 MiB of HBM per device.

```python
import math
import jax
import jax.numpy as jnp
import numpy as np
from jax import lax

D = 2048
HEADS = 8
HD = 128
FF = 1024
TOPK = 4
TOK_DEV = 256
TOKENS = 4096
EXPERTS = 16
CAP = 96
N_CTX = 16


def draw_tokens(key, part):
    row_key, column_key, normal_key = jax.random.split(key, 3)
    row_scale = jnp.exp(jax.random.uniform(row_key, (TOKENS, 1), jnp.float32, math.log(0.4), math.log(4.0)))
    column_scale = jnp.exp(jax.random.uniform(column_key, (1, D), jnp.float32, math.log(0.4), math.log(4.0)))
    drawn = jax.random.normal(normal_key, (TOKENS, D), jnp.float32)
    drawn = jnp.clip(drawn, -5.0, 5.0)
    return (drawn * row_scale * column_scale).astype(jnp.bfloat16)


def block_levels(stream_key, dims, cuts, smallest, high):
    factor_of = 1.0
    for axis_at, blocks in cuts:
        draws = jax.random.uniform(jax.random.fold_in(jax.random.fold_in(stream_key, 6), axis_at), (blocks,), jnp.float32, smallest / len(cuts), high / len(cuts))
        factor_of = factor_of * jnp.repeat(jnp.exp(draws), dims[axis_at] // blocks).reshape((-1,) + (1,) * (len(dims) - 1 - axis_at))
    return factor_of


def shared_out(stream_key, own, number, rows, count, top, bound, skew):
    order = jax.random.permutation(stream_key, count)
    heavy_load, usual = portions_of(count, rows * top, bound, skew, True), portions_of(count, rows * top, bound, skew, False)
    places = jnp.arange(count)

    def named(sizes, turn):
        used = int((sizes > 0).sum())
        fixed = max(1, used // 4)
        passed = fixed + (places - fixed + turn * (used - fixed)) % max(1, count - fixed)
        return jnp.zeros((count,), jnp.int32).at[order[jnp.where(places < fixed, places, passed)]].set(jnp.asarray(sizes, jnp.int32))

    sizes = jnp.where(number % 4 == 0, named(heavy_load, number // 4), named(usual, number - number // 4 - 1))
    mixed = jax.random.permutation(jax.random.fold_in(own, 3), count)
    giver, taker = mixed[0:count // 2 * 2:2], mixed[1:count // 2 * 2:2]
    slack = jnp.minimum(sizes[giver] - 1, bound - sizes[taker]) // 2
    slack = jnp.where((giver == order[0]) | (taker == order[0]) | (sizes[taker] == 0), 0, jnp.maximum(slack, 0))
    passed = jax.random.randint(jax.random.fold_in(own, 4), (count // 2,), 0, 1 << 20) % (slack + 1)
    sizes = sizes.at[giver].add(-passed).at[taker].add(passed)
    members = jnp.searchsorted(jnp.cumsum(sizes), jnp.arange(rows * top), side="right").astype(jnp.int32)
    table = members.reshape(top, rows).T
    table = table[jax.random.permutation(jax.random.fold_in(own, 1), rows)]
    turn = jax.random.randint(jax.random.fold_in(own, 2), (rows, 1), 0, top)
    return jnp.take_along_axis(table, (jnp.arange(top)[None, :] + turn) % top, axis=1)


def portions_of(number_of, total, bound, lean, full):
    loads = [(1 << 20) // math.isqrt(grade ** lean) + 1 for grade in range(1, number_of + 1)]
    largest = bound if full else min(bound, max(-(-total // number_of), total * loads[0] // sum(loads)))
    least = 1 if total - largest >= number_of - 1 else 0
    counts, rest = [largest] + [least] * (number_of - 1), total - largest - least * (number_of - 1)
    while rest > 0:
        movable = [i for i in range(1, number_of) if counts[i] < largest] or [i for i in range(1, number_of) if counts[i] < bound]
        pool, budget = sum([loads[i] for i in movable]), rest
        for i in movable:
            more = min(bound - counts[i], max(1, budget * loads[i] // pool), rest)
            counts[i] = counts[i] + more
            rest = rest - more
    return np.array(counts)


def normal_values(key, dims, width, reach, cuts=(), held_as=jnp.bfloat16):
    level = block_levels(key, dims, cuts, -0.22, 0.18) if cuts else 1.0
    result = jax.random.normal(key, dims, jnp.float32) * width * level
    return jnp.minimum(jnp.maximum(result, -reach), reach).astype(held_as)


def setup_inputs(seed: int = 0, part: int = 0) -> dict:
    keys = jax.random.split(jax.random.key(seed), 9)
    part_keys = jax.random.split(jax.random.fold_in(keys[8], part), 9)
    tokens = draw_tokens(jax.random.fold_in(jax.random.fold_in(keys[8], part), 71), part)
    qkv_weight = normal_values(keys[1], (D, 3 * HEADS * HD), D ** -0.5, 0.125, ((0, 16),))
    out_weight = normal_values(keys[2], (HEADS * HD, D), (HEADS * HD) ** -0.5, 0.1875, ((0, 16),))
    prior_state = normal_values(part_keys[3], (HEADS, HD, HD), 40.0, 240.0, (), jnp.float32)
    expert_ids_keys = jax.random.split(jax.random.fold_in(part_keys[4], 1), TOKENS // TOK_DEV)
    expert_ids_turns = jax.random.permutation(jax.random.fold_in(part_keys[4], 3), TOKENS // TOK_DEV)
    expert_ids = jax.vmap(lambda own, number: shared_out(jax.random.fold_in(part_keys[4], 2), own, number, TOK_DEV, EXPERTS, TOPK, CAP, 2))(expert_ids_keys, expert_ids_turns).reshape((TOKENS, TOPK))
    gate_weights = jnp.clip(0.1 + 0.9 * jax.random.uniform(part_keys[5], (TOKENS, TOPK), jnp.float32) ** block_levels(part_keys[5], (TOKENS, TOPK), ((0, 16),), -0.2, 0.2), 0.1, 1.0)
    expert_in = normal_values(keys[6], (EXPERTS, D, 2 * FF), D ** -0.5, 0.125, ((0, 16),))
    expert_out = normal_values(keys[7], (EXPERTS, FF, D), FF ** -0.5, 0.1875, ((0, 16),))
    return {"tokens": tokens, "qkv_weight": qkv_weight, "out_weight": out_weight, "prior_state": prior_state, "expert_ids": expert_ids, "gate_weights": gate_weights, "expert_in": expert_in, "expert_out": expert_out}


EPSILON = 1e-05

def rms_rows(matrix):
    return matrix * lax.rsqrt(lax.optimization_barrier(jnp.mean(matrix * matrix, axis=-1, keepdims=True)) + EPSILON)

def slot_places(chosen, experts, capacity):
    flat_ids = chosen.reshape(-1).astype(jnp.int32)
    onehot = (flat_ids[:, None] == jnp.arange(experts, dtype=jnp.int32)[None, :]).astype(jnp.int32)
    before = jnp.cumsum(onehot, axis=0) - onehot
    slot_index = lax.optimization_barrier(jnp.sum(before * onehot, axis=1)).astype(jnp.int32)
    return (flat_ids * capacity + slot_index).astype(jnp.int32)

def reference(tokens, qkv_weight, out_weight, prior_state, expert_ids, gate_weights, expert_in, expert_out):
    highest = lax.Precision.HIGHEST
    width_heads = HEADS * HD
    normed = rms_rows(tokens.astype(jnp.float32)).astype(jnp.bfloat16)
    projected = jnp.dot(normed, qkv_weight, preferred_element_type=jnp.float32)
    queries = jax.nn.silu(projected[:, :width_heads]).astype(jnp.bfloat16)
    key_rows = jax.nn.silu(projected[:, width_heads:2 * width_heads]).astype(jnp.bfloat16)
    value_rows = projected[:, 2 * width_heads:].astype(jnp.bfloat16)
    query_wide = queries.astype(jnp.float32).reshape(N_CTX, TOK_DEV, HEADS, HD)
    key_wide = key_rows.astype(jnp.float32).reshape(N_CTX, TOK_DEV, HEADS, HD)
    value_wide = value_rows.astype(jnp.float32).reshape(N_CTX, TOK_DEV, HEADS, HD)
    block_state = jnp.einsum('bthd,bthe->bhde', key_wide, value_wide, precision=highest)
    running_sum = jnp.cumsum(block_state, axis=0)
    earlier_sum = jnp.concatenate([jnp.zeros((1, HEADS, HD, HD), jnp.float32), running_sum[:-1]], axis=0)
    carried = prior_state[None] + earlier_sum
    scores = jnp.einsum('bthd,bshd->bhts', query_wide, key_wide, precision=highest)
    causal = jnp.arange(TOK_DEV, dtype=jnp.int32)[:, None] >= jnp.arange(TOK_DEV, dtype=jnp.int32)[None, :]
    scores = jnp.where(causal[None, None], scores, jnp.float32(0.0)).astype(jnp.bfloat16)
    scores = lax.optimization_barrier(scores).astype(jnp.float32)
    inside = jnp.einsum('bhts,bshe->bthe', scores, value_wide, precision=highest)
    from_state = jnp.einsum('bthd,bhde->bthe', query_wide, carried, precision=highest)
    head_normed = rms_rows(from_state + inside).astype(jnp.bfloat16).reshape(TOKENS, width_heads)
    attended = jnp.dot(head_normed, out_weight, preferred_element_type=jnp.float32)
    hidden = (tokens.astype(jnp.float32) + attended).astype(jnp.bfloat16)
    moe_in = rms_rows(hidden.astype(jnp.float32)).astype(jnp.bfloat16)
    places = jax.vmap(lambda chosen: slot_places(chosen, EXPERTS, CAP))(expert_ids.reshape(N_CTX, TOK_DEV, TOPK))
    repeated = jnp.repeat(moe_in.reshape(N_CTX, TOK_DEV, D), TOPK, axis=1)
    buffers = jax.vmap(lambda where_to, rows_in: jnp.zeros((EXPERTS * CAP, D), jnp.bfloat16).at[where_to].set(rows_in))(places, repeated)
    by_expert = buffers.reshape(N_CTX, EXPERTS, CAP, D).transpose(1, 0, 2, 3).reshape(EXPERTS, N_CTX * CAP, D)

    def run_expert(packed):
        rows_here, inner_weight, outer_weight = packed
        gate_up = jnp.dot(rows_here, inner_weight, preferred_element_type=jnp.float32)
        middle = (jax.nn.silu(gate_up[:, :FF]) * gate_up[:, FF:]).astype(jnp.bfloat16)
        return jnp.dot(middle, outer_weight, preferred_element_type=jnp.float32).astype(jnp.bfloat16)
    results = lax.map(run_expert, (by_expert, expert_in, expert_out))
    results = results.reshape(EXPERTS, N_CTX, CAP, D).transpose(1, 0, 2, 3).reshape(N_CTX, EXPERTS * CAP, D)
    picked = jax.vmap(lambda table_rows, where_to: table_rows[where_to])(results, places)
    picked = picked.reshape(TOKENS, TOPK, D).astype(jnp.float32)
    combined = lax.optimization_barrier(jnp.sum(gate_weights[:, :, None] * picked, axis=1))
    return (hidden.astype(jnp.float32) + combined).astype(jnp.bfloat16)
```

```python
import jax
import jax.numpy as jnp
from jax import lax
from jax.sharding import PartitionSpec as P

HEADS = 8
HD = 128
FF = 1024
SIDE = 4
GROUP = 4
EPSILON = 1e-05


def rms_rows(matrix):
    return matrix * lax.rsqrt(jnp.mean(matrix * matrix, axis=-1, keepdims=True) + EPSILON)


def swap_with(x, mask):
    return lax.ppermute(x, "dp", [(i, i ^ mask) for i in range(lax.axis_size("dp"))])


def shift_ctx(x, dx, dy):
    pairs = [
        (a * SIDE + b, (a + dx) % SIDE * SIDE + (b + dy) % SIDE)
        for a in range(SIDE)
        for b in range(SIDE)
    ]
    return lax.ppermute(x, "ctx", pairs)


def gather_by_exchange(x, axis):
    count = lax.axis_size(axis)
    spread = jnp.broadcast_to(x[None], (count,) + x.shape)
    return lax.all_to_all(spread, axis, split_axis=0, concat_axis=0, tiled=True)


def routing(expert_ids, gate_weights, experts, capacity):
    rows = expert_ids.shape[0]
    names = jnp.arange(experts, dtype=jnp.int32)
    hit = expert_ids[:, :, None] == names
    member = jnp.any(hit, axis=1)
    gate = jnp.sum(jnp.where(hit, gate_weights[:, :, None], 0.0), axis=1)
    order = jnp.arange(rows, dtype=jnp.int32)
    earlier = (order[:, None] > order[None, :]).astype(jnp.bfloat16)
    slot = jnp.dot(earlier, member.astype(jnp.bfloat16), preferred_element_type=jnp.float32)
    slot = jnp.where(member, slot.astype(jnp.int32), -1)
    slots = jnp.arange(capacity, dtype=jnp.int32)
    taken_out = slot.T[:, None, :] == slots[None, :, None]
    taken_back = slot[:, :, None] == slots[None, None, :]
    send = taken_out.astype(jnp.bfloat16).reshape(experts * capacity, rows)
    high = gate.astype(jnp.bfloat16)
    low = (gate - high.astype(jnp.float32)).astype(jnp.bfloat16)
    zero = jnp.zeros((), jnp.bfloat16)
    weigh = lambda g: jnp.where(taken_back, g[:, :, None], zero).reshape(rows, experts * capacity)
    return send, jnp.concatenate([weigh(high), weigh(low)], axis=0)


def shards(
    tokens, qkv_weight, out_weight, prior_state, expert_ids, gate_weights, expert_in, expert_out
):
    rows, width = tokens.shape
    width_heads = HEADS * HD
    experts = lax.axis_size("ctx")
    capacity = 3 * rows * expert_ids.shape[1] // (2 * experts)
    own_heads = HEADS // GROUP
    own_width = own_heads * HD
    place = lax.axis_index("dp") % GROUP
    column = lax.axis_index("ctx") // SIDE
    row = lax.axis_index("ctx") % SIDE

    part = lambda n: lax.dynamic_slice_in_dim(
        qkv_weight, n * width_heads + place * own_width, own_width, axis=1
    )
    own_weight = jnp.concatenate([part(0), part(1), part(2)], axis=1)

    out_full = lax.all_gather(out_weight, "ctx", axis=0, tiled=True)
    normed = rms_rows(tokens.astype(jnp.float32)).astype(jnp.bfloat16)
    far = swap_with(normed, 2)
    near = swap_with(normed, 1)
    prior = [lax.dynamic_slice_in_dim(prior_state, place * own_heads, own_heads, axis=0)]
    for other in range(1, GROUP):
        theirs = lax.dynamic_slice_in_dim(prior_state, (place ^ other) * own_heads, own_heads, axis=0)
        prior.append(swap_with(theirs, other))
    prior = jnp.stack(prior)
    weight = gather_by_exchange(own_weight, "ctx").reshape(width, 3 * own_width)
    diagonal = swap_with(far, 1)
    everyone = jnp.concatenate([normed, near, far, diagonal], axis=0)
    send, weigh = routing(expert_ids, gate_weights, experts, capacity)

    projected = jnp.dot(everyone, weight, preferred_element_type=jnp.float32)
    split = lambda m: m.astype(jnp.bfloat16).reshape(GROUP, rows, own_heads, HD)
    queries = split(jax.nn.silu(projected[:, :own_width]))
    key_rows = split(jax.nn.silu(projected[:, own_width : 2 * own_width]))
    value_rows = split(projected[:, 2 * own_width :])

    state = jnp.einsum(
        "jthd,jthe->jhde", key_rows, value_rows, preferred_element_type=jnp.float32
    )
    sent = state.astype(jnp.bfloat16)
    in_row = [shift_ctx(sent, 0, d).astype(jnp.float32) for d in range(1, SIDE)]
    total = (state + in_row[0] + in_row[1] + in_row[2]).astype(jnp.bfloat16)
    across = [shift_ctx(total, d, 0).astype(jnp.float32) for d in range(1, SIDE)]
    carried = prior
    for d in range(1, SIDE):
        carried = carried + jnp.where(row >= d, in_row[d - 1], 0.0)
        carried = carried + jnp.where(column >= d, across[d - 1], 0.0)

    scores = jnp.einsum("jthd,jshd->jhts", queries, key_rows, preferred_element_type=jnp.float32)
    order = jnp.arange(rows, dtype=jnp.int32)
    scores = jnp.where(order[:, None] >= order[None, :], scores, 0.0).astype(jnp.bfloat16)
    inside = jnp.einsum("jhts,jshe->jthe", scores, value_rows, preferred_element_type=jnp.float32)
    high = carried.astype(jnp.bfloat16)
    low = (carried - high.astype(jnp.float32)).astype(jnp.bfloat16)
    from_state = jnp.einsum(
        "jthd,jhde->jthe", queries, high, preferred_element_type=jnp.float32
    ) + jnp.einsum("jthd,jhde->jthe", queries, low, preferred_element_type=jnp.float32)
    head_normed = rms_rows(from_state + inside).astype(jnp.bfloat16)
    head_normed = head_normed.reshape(GROUP, rows, own_width)

    back = [head_normed[0]] + [swap_with(head_normed[j], j) for j in range(1, GROUP)]
    back = jnp.stack(back)
    ordered = [lax.dynamic_index_in_dim(back, b ^ place, 0, keepdims=False) for b in range(GROUP)]
    attended = jnp.dot(
        jnp.concatenate(ordered, axis=1), out_full, preferred_element_type=jnp.float32
    )
    hidden = (tokens.astype(jnp.float32) + attended).astype(jnp.bfloat16)
    moe_in = rms_rows(hidden.astype(jnp.float32)).astype(jnp.bfloat16)

    outgoing = jnp.dot(send, moe_in, preferred_element_type=jnp.float32).astype(jnp.bfloat16)
    outgoing = outgoing.reshape(experts, capacity, width)
    arrived = lax.all_to_all(outgoing, "ctx", split_axis=0, concat_axis=0, tiled=True)
    grouped = arrived.reshape(experts * capacity, width)
    gate_up = jnp.dot(grouped, expert_in[0], preferred_element_type=jnp.float32)
    middle = (jax.nn.silu(gate_up[:, :FF]) * gate_up[:, FF:]).astype(jnp.bfloat16)
    result = jnp.dot(middle, expert_out[0], preferred_element_type=jnp.float32).astype(jnp.bfloat16)
    returned = lax.all_to_all(
        result.reshape(experts, capacity, width), "ctx", split_axis=0, concat_axis=0, tiled=True
    ).reshape(experts * capacity, width)
    combined = jnp.dot(weigh, returned, preferred_element_type=jnp.float32)
    return (hidden.astype(jnp.float32) + (combined[:rows] + combined[rows:])).astype(jnp.bfloat16)


def solution(mesh):
    return jax.shard_map(
        shards,
        mesh=mesh,
        in_specs=(
            P(("dp", "ctx"), None),
            P("ctx", None),
            P("ctx", None),
            P("dp", None, None),
            P(("dp", "ctx"), None),
            P(("dp", "ctx"), None),
            P("ctx", None, None),
            P("ctx", None, None),
        ),
        out_specs=P(("dp", "ctx"), None),
        check_vma=False,
    )
```

```python
import jax
import jax.numpy as jnp
from jax import lax
from jax.experimental import pallas as pl
from jax.experimental.pallas import tpu as pltpu
from jax.sharding import PartitionSpec as P

HEADS = 8
HD = 128
FF = 1024
SIDE = 4
GROUP = 4
ROW_TILE = 512
VMEM_LIMIT = 36 << 20
EPSILON = 1e-05


def rms_rows(matrix):
    return matrix * lax.rsqrt(jnp.mean(matrix * matrix, axis=-1, keepdims=True) + EPSILON)


def swap_with(x, mask):
    return lax.ppermute(x, "dp", [(i, i ^ mask) for i in range(lax.axis_size("dp"))])


def shift_ctx(x, dx, dy):
    pairs = [
        (a * SIDE + b, (a + dx) % SIDE * SIDE + (b + dy) % SIDE)
        for a in range(SIDE)
        for b in range(SIDE)
    ]
    return lax.ppermute(x, "ctx", pairs)


def routing(expert_ids, gate_weights, experts, capacity):
    rows = expert_ids.shape[0]
    names = jnp.arange(experts, dtype=jnp.int32)
    hit = expert_ids[:, :, None] == names
    member = jnp.any(hit, axis=1)
    gate = jnp.sum(jnp.where(hit, gate_weights[:, :, None], 0.0), axis=1)
    order = jnp.arange(rows, dtype=jnp.int32)
    earlier = (order[:, None] > order[None, :]).astype(jnp.bfloat16)
    slot = jnp.dot(earlier, member.astype(jnp.bfloat16), preferred_element_type=jnp.float32)
    slot = jnp.where(member, slot.astype(jnp.int32), -1)
    slots = jnp.arange(capacity, dtype=jnp.int32)
    taken_out = slot.T[:, None, :] == slots[None, :, None]
    taken_back = slot[:, :, None] == slots[None, None, :]
    send = taken_out.astype(jnp.bfloat16).reshape(experts * capacity, rows)
    high = gate.astype(jnp.bfloat16)
    low = (gate - high.astype(jnp.float32)).astype(jnp.bfloat16)
    zero = jnp.zeros((), jnp.bfloat16)
    weigh = lambda g: jnp.where(taken_back, g[:, :, None], zero).reshape(rows, experts * capacity)
    return send, jnp.concatenate([weigh(high), weigh(low)], axis=0)


def dot32(a, b):
    return jnp.dot(a, b, preferred_element_type=jnp.float32)


def whole(a):
    return pl.BlockSpec(a.shape, lambda i: (0,) * a.ndim)


def one_of(a):
    return pl.BlockSpec((1,) + a.shape[1:], lambda i: (i,) + (0,) * (a.ndim - 1))


def call(kernel, name, grid, inputs, in_specs, outputs, out_specs, flops, scratch=()):
    size = lambda a: a.size * a.dtype.itemsize
    return pl.pallas_call(
        kernel,
        grid=(grid,),
        in_specs=in_specs,
        out_specs=out_specs,
        out_shape=outputs,
        scratch_shapes=list(scratch),
        compiler_params=pltpu.CompilerParams(vmem_limit_bytes=VMEM_LIMIT),
        cost_estimate=pl.CostEstimate(
            flops=flops,
            bytes_accessed=sum(size(a) for a in inputs) + sum(size(a) for a in outputs),
            transcendentals=0,
        ),
        name=name,
    )(*inputs)


def out_like(shape, dtype):
    return jax.ShapeDtypeStruct(shape, dtype)


def key_value_kernel(w_ref, *refs):
    rows_refs, (pair_ref, state_ref, sent_ref) = refs[:GROUP], refs[GROUP:]
    own_width = w_ref.shape[1] // 2
    for j, x_ref in enumerate(rows_refs):

        @pl.when(pl.program_id(0) == j)
        def _(x_ref=x_ref):
            both = dot32(x_ref[...], w_ref[...])
            keys = jax.nn.silu(both[:, :own_width]).astype(jnp.bfloat16)
            values = both[:, own_width:].astype(jnp.bfloat16)
            pair_ref[0, :, :own_width] = keys
            pair_ref[0, :, own_width:] = values
            for h in range(own_width // HD):
                cut = slice(h * HD, (h + 1) * HD)
                state = lax.dot_general(
                    keys[:, cut],
                    values[:, cut],
                    (((0,), (0,)), ((), ())),
                    preferred_element_type=jnp.float32,
                )
                state_ref[0, h] = state
                sent_ref[0, h] = state.astype(jnp.bfloat16)


def keys_values_states(weight, everyone):
    rows, width = everyone[0].shape
    columns = weight.shape[1]
    heads = columns // 2 // HD
    pair = out_like((GROUP, rows, columns), jnp.bfloat16)
    state = out_like((GROUP, heads, HD, HD), jnp.float32)
    sent = out_like((GROUP, heads, HD, HD), jnp.bfloat16)
    inputs = [weight, *everyone]
    outputs = [pair, state, sent]
    flops = 2 * GROUP * rows * width * columns
    return call(
        key_value_kernel, "keys_values_states", GROUP, inputs, [whole(a) for a in inputs],
        outputs, [one_of(a) for a in outputs], flops,
    )


def query_kernel(w_ref, pair_ref, *refs):
    rows_refs, (query_ref, inside_ref) = refs[:GROUP], refs[GROUP:]
    own_width = w_ref.shape[1]
    rows = pair_ref.shape[1]
    for j, x_ref in enumerate(rows_refs):

        @pl.when(pl.program_id(0) == j)
        def _(x_ref=x_ref):
            query_ref[0] = jax.nn.silu(dot32(x_ref[...], w_ref[...])).astype(jnp.bfloat16)

    causal = lax.broadcasted_iota(jnp.int32, (rows, rows), 0) >= lax.broadcasted_iota(
        jnp.int32, (rows, rows), 1
    )
    for h in range(own_width // HD):
        keys = pair_ref[0, :, h * HD : (h + 1) * HD]
        values = pair_ref[0, :, own_width + h * HD : own_width + (h + 1) * HD]
        scores = lax.dot_general(
            query_ref[0, :, h * HD : (h + 1) * HD],
            keys,
            (((1,), (1,)), ((), ())),
            preferred_element_type=jnp.float32,
        )
        scores = jnp.where(causal, scores, 0.0).astype(jnp.bfloat16)
        inside_ref[0, :, h * HD : (h + 1) * HD] = dot32(scores, values)


def queries_inside(weight, pair, everyone):
    rows, width = everyone[0].shape
    own_width = weight.shape[1]
    inputs = [weight, pair, *everyone]
    outputs = [
        out_like((GROUP, rows, own_width), jnp.bfloat16),
        out_like((GROUP, rows, own_width), jnp.float32),
    ]
    flops = 2 * GROUP * rows * own_width * (width + 2 * rows)
    return call(
        query_kernel, "queries_inside", GROUP, inputs,
        [whole(weight), one_of(pair)] + [whole(a) for a in everyone],
        outputs, [one_of(a) for a in outputs], flops,
    )


def finish_kernel(where_ref, query_ref, inside_ref, base_ref, *refs):
    across, out_ref = refs[:-1], refs[-1]
    for h in range(base_ref.shape[1]):
        carried = base_ref[0, h]
        for d, ref in enumerate(across):
            reached = (where_ref[0] > d).astype(jnp.float32)
            carried = carried + ref[0, h].astype(jnp.float32) * reached
        high = carried.astype(jnp.bfloat16)
        low = (carried - high.astype(jnp.float32)).astype(jnp.bfloat16)
        cut = slice(h * HD, (h + 1) * HD)
        query = query_ref[0, :, cut]
        mixed = dot32(query, high) + dot32(query, low) + inside_ref[0, :, cut]
        out_ref[0, :, cut] = rms_rows(mixed).astype(jnp.bfloat16)


def finished_heads(column, query, inside, base, across):
    inputs = [column.reshape(1), query, inside, base, *across]
    specs = [pl.BlockSpec(memory_space=pltpu.SMEM)] + [one_of(a) for a in inputs[1:]]
    output = out_like(query.shape, jnp.bfloat16)
    return call(
        finish_kernel, "finished_heads", GROUP, inputs, specs, [output], [one_of(output)],
        4 * query.size * HD,
    )[0]


def project_kernel(where_ref, tokens_ref, send_ref, *refs):
    back, quarters = refs[:GROUP], refs[GROUP : 2 * GROUP]
    hidden_ref, rows_ref, ordered_ref, sum_ref, normed_ref = refs[2 * GROUP :]
    own_width = back[0].shape[1]
    count, twice, narrow = quarters[0].shape
    half = twice // 2

    @pl.when(pl.program_id(0) == 0)
    def _():
        for j, ref in enumerate(back):
            at = pl.multiple_of((where_ref[0] ^ j) * own_width, own_width)
            ordered_ref[:, pl.ds(at, own_width)] = ref[...]
        heads = ordered_ref[...]
        for j, ref in enumerate(quarters):
            for n in range(2):
                weight = ref[:, n * half : (n + 1) * half, :].reshape(count * half, narrow)
                at = pl.multiple_of(((where_ref[0] ^ j) * 2 + n) * narrow, narrow)
                sum_ref[:, pl.ds(at, narrow)] = dot32(heads, weight)
        hidden = (tokens_ref[...].astype(jnp.float32) + sum_ref[...]).astype(jnp.bfloat16)
        hidden_ref[...] = hidden
        normed_ref[...] = rms_rows(hidden.astype(jnp.float32)).astype(jnp.bfloat16)

    rows_ref[...] = dot32(send_ref[...], normed_ref[...]).astype(jnp.bfloat16)


def projected_rows(place, tokens, send, back, quarters):
    rows, width = tokens.shape
    slots = send.shape[0]
    tile = slots // 4
    inputs = [place.reshape(1), tokens, send, *back, *quarters]
    specs = [pl.BlockSpec(memory_space=pltpu.SMEM), whole(tokens)]
    specs += [pl.BlockSpec((tile, rows), lambda i: (i, 0))]
    specs += [whole(a) for a in inputs[3:]]
    outputs = [out_like((rows, width), jnp.bfloat16), out_like((slots, width), jnp.bfloat16)]
    out_specs = [whole(outputs[0]), pl.BlockSpec((tile, width), lambda i: (i, 0))]
    scratch = [
        pltpu.VMEM((rows, GROUP * back[0].shape[1]), jnp.bfloat16),
        pltpu.VMEM((rows, width), jnp.float32),
        pltpu.VMEM((rows, width), jnp.bfloat16),
    ]
    flops = 2 * rows * width * (slots + GROUP * back[0].shape[1])
    return call(project_kernel, "projected_rows", 4, inputs, specs, outputs, out_specs, flops, scratch)


def expert_kernel(rows_ref, gate_ref, up_ref, out_weight_ref, out_ref, middle_ref):
    step = pl.program_id(0)
    inner = gate_ref.shape[1]
    chunks = FF // inner
    tile = ROW_TILE
    tiles = rows_ref.shape[0] // tile

    @pl.when(step < chunks)
    def _():
        at = pl.multiple_of(step * inner, inner)
        for r in range(tiles):
            cut = slice(r * tile, (r + 1) * tile)
            gate = dot32(rows_ref[cut, :], gate_ref[...])
            up = dot32(rows_ref[cut, :], up_ref[...])
            middle_ref[cut, pl.ds(at, inner)] = (jax.nn.silu(gate) * up).astype(jnp.bfloat16)

    @pl.when(step >= chunks)
    def _():
        for r in range(tiles):
            cut = slice(r * tile, (r + 1) * tile)
            out_ref[cut, :] = dot32(middle_ref[cut, :], out_weight_ref[...]).astype(jnp.bfloat16)


def expert_rows(rows, inner_weight, outer_weight):
    count, width = rows.shape
    chunks, inner, outer = FF // 256, 256, 512
    last = chunks - 1
    inputs = [rows, inner_weight, inner_weight, outer_weight]
    output = out_like((count, width), jnp.bfloat16)
    specs = [
        whole(rows),
        pl.BlockSpec((width, inner), lambda i: (0, jnp.minimum(i, last))),
        pl.BlockSpec((width, inner), lambda i: (0, chunks + jnp.minimum(i, last))),
        pl.BlockSpec((FF, outer), lambda i: (0, jnp.maximum(i - chunks, 0))),
    ]
    out_spec = pl.BlockSpec((count, outer), lambda i: (0, jnp.maximum(i - chunks, 0)))
    return call(
        expert_kernel, "expert_rows", chunks + width // outer, inputs, specs, [output], [out_spec],
        2 * count * width * 3 * FF, [pltpu.VMEM((count, FF), jnp.bfloat16)],
    )[0]


def shards(
    tokens, qkv_weight, out_weight, prior_state, expert_ids, gate_weights, expert_in, expert_out
):
    rows, width = tokens.shape
    width_heads = HEADS * HD
    experts = lax.axis_size("ctx")
    capacity = 3 * rows * expert_ids.shape[1] // (2 * experts)
    own_heads = HEADS // GROUP
    own_width = own_heads * HD
    place = lax.axis_index("dp") % GROUP
    column = lax.axis_index("ctx") // SIDE
    row = lax.axis_index("ctx") % SIDE
    cut = lambda a, start, size, axis: lax.dynamic_slice_in_dim(a, start, size, axis=axis)
    shard_rows = qkv_weight.shape[0]

    part = lambda n: cut(qkv_weight, n * width_heads + place * own_width, own_width, 1)
    first = jnp.concatenate([part(1), part(2)], axis=1)
    out_part = cut(out_weight, place * (width // GROUP), width // GROUP, 1)
    out_parts = jnp.split(out_part, width // GROUP // own_width, axis=1)
    second = jnp.concatenate([part(0)] + out_parts, axis=0)
    second = lax.all_gather(second[None], "ctx", axis=0, tiled=True)

    spread = jnp.broadcast_to(first[None], (experts,) + first.shape)
    spread, tokens = lax.optimization_barrier((spread, tokens))
    normed = rms_rows(tokens.astype(jnp.float32)).astype(jnp.bfloat16)
    far = swap_with(normed, 2)
    near = swap_with(normed, 1)
    first = lax.all_to_all(spread, "ctx", split_axis=0, concat_axis=0, tiled=True)
    everyone = [normed, near, far, swap_with(far, 1)]
    prior = [cut(prior_state, place * own_heads, own_heads, 0)]
    for other in range(1, GROUP):
        prior.append(swap_with(cut(prior_state, (place ^ other) * own_heads, own_heads, 0), other))
    first, prior = lax.optimization_barrier((first, tuple(prior)))
    prior = jnp.stack(prior)

    pair, state, sent = keys_values_states(first.reshape(width, 2 * own_width), everyone)
    in_row = [shift_ctx(sent, 0, d).astype(jnp.float32) for d in range(1, SIDE)]
    total = (state + in_row[0] + in_row[1] + in_row[2]).astype(jnp.bfloat16)
    base = prior
    for d in range(1, SIDE):
        base = base + jnp.where(row >= d, in_row[d - 1], 0.0)

    second, total = lax.optimization_barrier((second, total))
    across = [shift_ctx(total, d, 0) for d in range(1, SIDE)]
    query, inside = queries_inside(second[:, :shard_rows].reshape(width, own_width), pair, everyone)
    quarter = second[:, shard_rows:]
    quarter_far = swap_with(quarter, 2)
    quarter_near = swap_with(quarter, 1)
    send, weigh = routing(expert_ids, gate_weights, experts, capacity)

    head_normed = finished_heads(column, query, inside, base, across)
    quarter_far, head_normed = lax.optimization_barrier((quarter_far, head_normed))
    quarters = [quarter, quarter_near, quarter_far, swap_with(quarter_far, 1)]
    back = [head_normed[0]] + [swap_with(head_normed[j], j) for j in range(1, GROUP)]
    hidden, outgoing = projected_rows(place, tokens, send, back, quarters)

    outgoing, weigh, hidden = lax.optimization_barrier((outgoing, weigh, hidden))
    outgoing = outgoing.reshape(experts, capacity, width)
    arrived = lax.all_to_all(outgoing, "ctx", split_axis=0, concat_axis=0, tiled=True)
    grouped = arrived.reshape(experts * capacity, width)
    result = expert_rows(grouped, expert_in[0], expert_out[0])
    result, weigh, hidden = lax.optimization_barrier((result, weigh, hidden))
    returned = lax.all_to_all(
        result.reshape(experts, capacity, width), "ctx", split_axis=0, concat_axis=0, tiled=True
    ).reshape(experts * capacity, width)
    combined = jnp.dot(weigh, returned, preferred_element_type=jnp.float32)
    return (hidden.astype(jnp.float32) + (combined[:rows] + combined[rows:])).astype(jnp.bfloat16)


def solution(mesh):
    return jax.shard_map(
        shards,
        mesh=mesh,
        in_specs=(
            P(("dp", "ctx"), None),
            P("ctx", None),
            P("ctx", None),
            P("dp", None, None),
            P(("dp", "ctx"), None),
            P(("dp", "ctx"), None),
            P("ctx", None, None),
            P("ctx", None, None),
        ),
        out_specs=P(("dp", "ctx"), None),
        check_vma=False,
    )
```

```python
import jax
import jax.numpy as jnp
from jax import lax
from jax.experimental import pallas as pl
from jax.experimental.pallas import tpu as pltpu
from jax.sharding import PartitionSpec as P

HEADS = 8
HD = 128
FF = 1024
SIDE = 4
GROUP = 4
ROW_TILE = 512
VMEM_LIMIT = 36 << 20
HIGH_VMEM_LIMIT = 58 << 20
EPSILON = 1e-05


def rms_rows(matrix):
    return matrix * lax.rsqrt(jnp.mean(matrix * matrix, axis=-1, keepdims=True) + EPSILON)


def swap_with(x, mask):
    return lax.ppermute(x, "dp", [(i, i ^ mask) for i in range(lax.axis_size("dp"))])


def shift_ctx(x, dx, dy):
    pairs = [
        (a * SIDE + b, (a + dx) % SIDE * SIDE + (b + dy) % SIDE)
        for a in range(SIDE)
        for b in range(SIDE)
    ]
    return lax.ppermute(x, "ctx", pairs)


def routing(expert_ids, gate_weights, experts, capacity):
    rows = expert_ids.shape[0]
    names = jnp.arange(experts, dtype=jnp.int32)
    hit = expert_ids[:, :, None] == names
    member = jnp.any(hit, axis=1)
    gate = jnp.sum(jnp.where(hit, gate_weights[:, :, None], 0.0), axis=1)
    order = jnp.arange(rows, dtype=jnp.int32)
    earlier = (order[:, None] > order[None, :]).astype(jnp.bfloat16)
    slot = jnp.dot(earlier, member.astype(jnp.bfloat16), preferred_element_type=jnp.float32)
    slot = jnp.where(member, slot.astype(jnp.int32), -1)
    slots = jnp.arange(capacity, dtype=jnp.int32)
    taken = slot.T[:, None, :] == slots[None, :, None]
    send = taken.astype(jnp.bfloat16).reshape(experts * capacity, rows)
    taken_back = slot[:, :, None] == slots[None, None, :]
    high = gate.astype(jnp.bfloat16)
    low = (gate - high.astype(jnp.float32)).astype(jnp.bfloat16)
    zero = jnp.zeros((), jnp.bfloat16)
    weigh = lambda g: jnp.where(taken_back, g[:, :, None], zero).reshape(rows, experts * capacity)
    return send, jnp.concatenate([weigh(high), weigh(low)], axis=0)


def dot32(a, b):
    return jnp.dot(a, b, preferred_element_type=jnp.float32)


def whole(a):
    return pl.BlockSpec(a.shape, lambda i: (0,) * a.ndim)


def slab_of(a, n):
    return pl.BlockSpec((a.shape[0], 128, a.shape[2]), lambda i: (0, n, 0))


def one_of(a):
    return pl.BlockSpec((1,) + a.shape[1:], lambda i: (i,) + (0,) * (a.ndim - 1))


def call(kernel, name, grid, inputs, in_specs, outputs, out_specs, flops, scratch=(), aliases={}, limit=VMEM_LIMIT):
    size = lambda a: a.size * a.dtype.itemsize
    return pl.pallas_call(
        kernel,
        grid=(grid,),
        in_specs=in_specs,
        out_specs=out_specs,
        out_shape=outputs,
        scratch_shapes=list(scratch),
        input_output_aliases=aliases,
        compiler_params=pltpu.CompilerParams(vmem_limit_bytes=limit),
        cost_estimate=pl.CostEstimate(
            flops=flops,
            bytes_accessed=sum(size(a) for a in inputs) + sum(size(a) for a in outputs),
            transcendentals=0,
        ),
        name=name,
    )(*inputs)


def out_like(shape, dtype):
    return jax.ShapeDtypeStruct(shape, dtype)


def prepare_kernel(where_ref, tokens_ref, qkv_ref, out_ref, spread_ref, second_ref, normed_ref):
    own_width = second_ref.shape[1]
    width_heads = HEADS * HD
    shard_rows = qkv_ref.shape[0]
    share = out_ref.shape[1] // 2
    at = lambda start, size: pl.ds(pl.multiple_of(start, size), size)
    part = lambda n: qkv_ref[:, at(n * width_heads + where_ref[0] * own_width, own_width)]
    normed_ref[...] = rms_rows(tokens_ref[...].astype(jnp.float32)).astype(jnp.bfloat16)
    keys, values = part(1), part(2)
    for n in range(spread_ref.shape[0]):
        spread_ref[n, :, :own_width] = keys
        spread_ref[n, :, own_width:] = values

    @pl.when(pl.program_id(0) == 0)
    def _():
        second_ref[:shard_rows] = part(0)
        rows = out_ref.shape[0]
        for n in range(share // own_width):
            columns = at((where_ref[0] & 1) * share + n * own_width, own_width)
            second_ref[shard_rows + n * rows : shard_rows + (n + 1) * rows] = out_ref[:, columns]


def prepared(place, tokens, qkv_weight, out_weight, own_width, experts):
    steps = 4
    rows, width = tokens.shape
    stacked = qkv_weight.shape[0] + out_weight.shape[0] * (width // 2 // own_width)
    inputs = [place.reshape(1), tokens, qkv_weight, out_weight]
    outputs = [
        out_like((experts, qkv_weight.shape[0], 2 * own_width), jnp.bfloat16),
        out_like((stacked, own_width), jnp.bfloat16),
        out_like((rows, width), jnp.bfloat16),
    ]
    slab = lambda a: pl.BlockSpec((a.shape[0] // steps,) + a.shape[1:], lambda i: (i,) + (0,) * (a.ndim - 1))
    return call(
        prepare_kernel, "prepared", steps, inputs,
        [pl.BlockSpec(memory_space=pltpu.SMEM), slab(tokens), whole(qkv_weight), whole(out_weight)],
        outputs, [slab(outputs[0]), whole(outputs[1]), slab(outputs[2])], 4 * tokens.size,
        limit=HIGH_VMEM_LIMIT,
    )


def key_value_kernel(w_ref, *refs):
    rows_refs, (pair_ref, state_ref, sent_ref) = refs[:GROUP], refs[GROUP:]
    own_width = w_ref.shape[1] // 2
    for j, x_ref in enumerate(rows_refs):

        @pl.when(pl.program_id(0) == j)
        def _(x_ref=x_ref):
            both = dot32(x_ref[...], w_ref[...])
            keys = jax.nn.silu(both[:, :own_width]).astype(jnp.bfloat16)
            values = both[:, own_width:].astype(jnp.bfloat16)
            pair_ref[0, :, :own_width] = keys
            pair_ref[0, :, own_width:] = values
            for h in range(own_width // HD):
                cut = slice(h * HD, (h + 1) * HD)
                state = lax.dot_general(
                    keys[:, cut],
                    values[:, cut],
                    (((0,), (0,)), ((), ())),
                    preferred_element_type=jnp.float32,
                )
                state_ref[0, h] = state
                sent_ref[0, h] = state.astype(jnp.bfloat16)


def keys_values_states(weight, everyone):
    rows, width = everyone[0].shape
    columns = weight.shape[1]
    heads = columns // 2 // HD
    pair = out_like((GROUP, rows, columns), jnp.bfloat16)
    state = out_like((GROUP, heads, HD, HD), jnp.float32)
    sent = out_like((GROUP, heads, HD, HD), jnp.bfloat16)
    inputs = [weight, *everyone]
    outputs = [pair, state, sent]
    flops = 2 * GROUP * rows * width * columns
    return call(
        key_value_kernel, "keys_values_states", GROUP, inputs, [whole(a) for a in inputs],
        outputs, [one_of(a) for a in outputs], flops,
    )


def query_kernel(w_ref, pair_ref, *refs):
    rows_refs, (query_ref, inside_ref) = refs[:GROUP], refs[GROUP:]
    own_width = w_ref.shape[2]
    rows = pair_ref.shape[1]
    for j, x_ref in enumerate(rows_refs):

        @pl.when(pl.program_id(0) == j)
        def _(x_ref=x_ref):
            weight = w_ref[...].reshape(-1, own_width)
            query_ref[0] = jax.nn.silu(dot32(x_ref[...], weight)).astype(jnp.bfloat16)

    causal = lax.broadcasted_iota(jnp.int32, (rows, rows), 0) >= lax.broadcasted_iota(
        jnp.int32, (rows, rows), 1
    )
    for h in range(own_width // HD):
        keys = pair_ref[0, :, h * HD : (h + 1) * HD]
        values = pair_ref[0, :, own_width + h * HD : own_width + (h + 1) * HD]
        scores = lax.dot_general(
            query_ref[0, :, h * HD : (h + 1) * HD],
            keys,
            (((1,), (1,)), ((), ())),
            preferred_element_type=jnp.float32,
        )
        scores = jnp.where(causal, scores, 0.0).astype(jnp.bfloat16)
        inside_ref[0, :, h * HD : (h + 1) * HD] = dot32(scores, values)


def queries_inside(weight, pair, everyone):
    rows, width = everyone[0].shape
    own_width = weight.shape[2]
    inputs = [weight, pair, *everyone]
    outputs = [
        out_like((GROUP, rows, own_width), jnp.bfloat16),
        out_like((GROUP, rows, own_width), jnp.float32),
    ]
    flops = 2 * GROUP * rows * own_width * (width + 2 * rows)
    return call(
        query_kernel, "queries_inside", GROUP, inputs,
        [slab_of(weight, 0), one_of(pair)] + [whole(a) for a in everyone],
        outputs, [one_of(a) for a in outputs], flops,
    )


def finish_kernel(where_ref, query_ref, inside_ref, base_ref, *refs):
    across, out_ref = refs[:-1], refs[-1]
    for h in range(base_ref.shape[1]):
        carried = base_ref[0, h]
        for d, ref in enumerate(across):
            reached = (where_ref[0] > d).astype(jnp.float32)
            carried = carried + ref[0, h].astype(jnp.float32) * reached
        high = carried.astype(jnp.bfloat16)
        low = (carried - high.astype(jnp.float32)).astype(jnp.bfloat16)
        cut = slice(h * HD, (h + 1) * HD)
        query = query_ref[0, :, cut]
        mixed = dot32(query, high) + dot32(query, low) + inside_ref[0, :, cut]
        out_ref[0, :, cut] = rms_rows(mixed).astype(jnp.bfloat16)


def finished_heads(column, query, inside, base, across):
    inputs = [column.reshape(1), query, inside, base, *across]
    specs = [pl.BlockSpec(memory_space=pltpu.SMEM)] + [one_of(a) for a in inputs[1:]]
    output = out_like(query.shape, jnp.bfloat16)
    return call(
        finish_kernel, "finished_heads", GROUP, inputs, specs, [output], [one_of(output)],
        4 * query.size * HD,
    )[0]


def project_kernel(where_ref, tokens_ref, send_ref, *refs):
    back, slabs = refs[:GROUP], refs[GROUP : GROUP + 4]
    hidden_ref, rows_ref, ordered_ref, sum_ref, normed_ref = refs[GROUP + 4 :]
    own_width = back[0].shape[1]
    count, stacked, narrow = slabs[0].shape
    shard = ordered_ref.shape[1] // count
    parts = stacked // shard
    step = pl.program_id(0)

    @pl.when(step == 0)
    def _():
        for j, ref in enumerate(back):
            at = pl.multiple_of((where_ref[0] ^ j) * own_width, own_width)
            ordered_ref[:, pl.ds(at, own_width)] = ref[...]
        heads = ordered_ref[...]
        for j, ref in enumerate(slabs):
            for n in range(parts):
                weight = ref[:, n * shard : (n + 1) * shard, :].reshape(count * shard, narrow)
                at = ((where_ref[0] & 1) ^ (j // 2)) * 2 * parts + j % 2 * parts + n
                at = pl.multiple_of(at * narrow, narrow)
                sum_ref[:, pl.ds(at, narrow)] = dot32(heads, weight)
        hidden = (tokens_ref[...].astype(jnp.float32) + sum_ref[...]).astype(jnp.bfloat16)
        hidden_ref[...] = hidden
        normed_ref[...] = rms_rows(hidden.astype(jnp.float32)).astype(jnp.bfloat16)

    rows_ref[...] = dot32(send_ref[...], normed_ref[...]).astype(jnp.bfloat16)


def projected_rows(place, tokens, send, back, halves):
    rows, width = tokens.shape
    slots = send.shape[0]
    tile = 384
    inputs = [place.reshape(1), tokens, send, *back, halves[0], halves[0], halves[1], halves[1]]
    specs = [pl.BlockSpec(memory_space=pltpu.SMEM), whole(tokens)]
    specs += [pl.BlockSpec((tile, rows), lambda i: (i, 0))]
    specs += [whole(a) for a in back] + [slab_of(a, n) for a in halves for n in (1, 2)]
    outputs = [
        out_like((rows, width), jnp.bfloat16),
        out_like((slots, width), jnp.bfloat16),
    ]
    out_specs = [
        whole(outputs[0]),
        pl.BlockSpec((tile, width), lambda i: (i, 0)),
    ]
    scratch = [
        pltpu.VMEM((rows, GROUP * back[0].shape[1]), jnp.bfloat16),
        pltpu.VMEM((rows, width), jnp.float32),
        pltpu.VMEM((rows, width), jnp.bfloat16),
    ]
    flops = 2 * rows * width * (slots + GROUP * back[0].shape[1])
    return call(
        project_kernel, "projected_rows", slots // tile, inputs, specs, outputs, out_specs, flops, scratch
    )


def expert_kernel(rows_ref, gate_ref, up_ref, out_weight_ref, out_ref, middle_ref):
    step = pl.program_id(0)
    inner = gate_ref.shape[1]
    chunks = FF // inner
    tile = ROW_TILE
    tiles = rows_ref.shape[0] // tile

    @pl.when(step < chunks)
    def _():
        at = pl.multiple_of(step * inner, inner)
        for r in range(tiles):
            cut = slice(r * tile, (r + 1) * tile)
            gate = dot32(rows_ref[cut, :], gate_ref[...])
            up = dot32(rows_ref[cut, :], up_ref[...])
            middle_ref[cut, pl.ds(at, inner)] = (jax.nn.silu(gate) * up).astype(jnp.bfloat16)

    @pl.when(step >= chunks)
    def _():
        for r in range(tiles):
            cut = slice(r * tile, (r + 1) * tile)
            out_ref[cut, :] = dot32(middle_ref[cut, :], out_weight_ref[...]).astype(jnp.bfloat16)


def expert_rows(rows, inner_weight, outer_weight):
    count, width = rows.shape
    chunks, inner, outer = FF // 256, 256, 512
    last = chunks - 1
    inputs = [rows, inner_weight, inner_weight, outer_weight]
    output = out_like((count, width), jnp.bfloat16)
    specs = [
        whole(rows),
        pl.BlockSpec((width, inner), lambda i: (0, jnp.minimum(i, last))),
        pl.BlockSpec((width, inner), lambda i: (0, chunks + jnp.minimum(i, last))),
        pl.BlockSpec((FF, outer), lambda i: (0, jnp.maximum(i - chunks, 0))),
    ]
    out_spec = pl.BlockSpec((count, outer), lambda i: (0, jnp.maximum(i - chunks, 0)))
    return call(
        expert_kernel, "expert_rows", chunks + width // outer, inputs, specs, [output], [out_spec],
        2 * count * width * 3 * FF, [pltpu.VMEM((count, FF), jnp.bfloat16)],
    )[0]


def shards(
    tokens, qkv_weight, out_weight, prior_state, expert_ids, gate_weights, expert_in, expert_out
):
    rows, width = tokens.shape
    width_heads = HEADS * HD
    experts = lax.axis_size("ctx")
    capacity = 3 * rows * expert_ids.shape[1] // (2 * experts)
    own_heads = HEADS // GROUP
    own_width = own_heads * HD
    place = lax.axis_index("dp") % GROUP
    column = lax.axis_index("ctx") // SIDE
    row = lax.axis_index("ctx") % SIDE
    cut = lambda a, start, size, axis: lax.dynamic_slice_in_dim(a, start, size, axis=axis)

    spread, second, normed = prepared(place, tokens, qkv_weight, out_weight, own_width, experts)
    second = lax.all_gather(second[None], "ctx", axis=0, tiled=True)
    far = swap_with(normed, 2)
    near = swap_with(normed, 1)
    first = lax.all_to_all(spread, "ctx", split_axis=0, concat_axis=0, tiled=True)
    everyone = [normed, near, far, swap_with(far, 1)]
    prior = [cut(prior_state, place * own_heads, own_heads, 0)]
    for other in range(1, GROUP):
        prior.append(swap_with(cut(prior_state, (place ^ other) * own_heads, own_heads, 0), other))
    send, weigh = routing(expert_ids, gate_weights, experts, capacity)
    first, prior, send, weigh = lax.optimization_barrier((first, tuple(prior), send, weigh))
    prior = jnp.stack(prior)

    pair, state, sent = keys_values_states(first.reshape(width, 2 * own_width), everyone)
    in_row = [shift_ctx(sent, 0, d).astype(jnp.float32) for d in range(1, SIDE)]
    total = (state + in_row[0] + in_row[1] + in_row[2]).astype(jnp.bfloat16)
    base = prior
    for d in range(1, SIDE):
        base = base + jnp.where(row >= d, in_row[d - 1], 0.0)

    second, _ = lax.optimization_barrier((second, total))
    across = [shift_ctx(total, d, 0) for d in range(1, SIDE)]
    query, inside = queries_inside(second, pair, everyone)
    halves = [second, swap_with(second, 1)]

    head_normed = finished_heads(column, query, inside, base, across)
    back = [head_normed[0]] + [swap_with(head_normed[j], j) for j in range(1, GROUP)]
    hidden, outgoing = projected_rows(place, tokens, send, back, halves)

    outgoing, weigh, hidden = lax.optimization_barrier((outgoing, weigh, hidden))
    outgoing = outgoing.reshape(experts, capacity, width)
    arrived = lax.all_to_all(outgoing, "ctx", split_axis=0, concat_axis=0, tiled=True)
    grouped = arrived.reshape(experts * capacity, width)
    result = expert_rows(grouped, expert_in[0], expert_out[0])
    result, weigh, hidden = lax.optimization_barrier((result, weigh, hidden))
    returned = lax.all_to_all(
        result.reshape(experts, capacity, width), "ctx", split_axis=0, concat_axis=0, tiled=True
    ).reshape(experts * capacity, width)
    combined = jnp.dot(weigh, returned, preferred_element_type=jnp.float32)
    return (hidden.astype(jnp.float32) + (combined[:rows] + combined[rows:])).astype(jnp.bfloat16)


def solution(mesh):
    return jax.shard_map(
        shards,
        mesh=mesh,
        in_specs=(
            P(("dp", "ctx"), None),
            P("ctx", None),
            P("ctx", None),
            P("dp", None, None),
            P(("dp", "ctx"), None),
            P(("dp", "ctx"), None),
            P("ctx", None, None),
            P("ctx", None, None),
        ),
        out_specs=P(("dp", "ctx"), None),
        check_vma=False,
    )
```

```python
import jax
import jax.numpy as jnp
from jax import lax
from jax.experimental import pallas as pl
from jax.experimental.pallas import tpu as pltpu
from jax.sharding import PartitionSpec as P

HEADS = 8
HD = 128
FF = 1024
SIDE = 4
GROUP = 4
ROW_TILE = 512
VMEM_LIMIT = 36 << 20
HIGH_VMEM_LIMIT = 58 << 20
EPSILON = 1e-05


def rms_rows(matrix):
    return matrix * lax.rsqrt(jnp.mean(matrix * matrix, axis=-1, keepdims=True) + EPSILON)


def swap_with(x, mask):
    return lax.ppermute(x, "dp", [(i, i ^ mask) for i in range(lax.axis_size("dp"))])


def shift_ctx(x, dx, dy):
    pairs = [
        (a * SIDE + b, (a + dx) % SIDE * SIDE + (b + dy) % SIDE)
        for a in range(SIDE)
        for b in range(SIDE)
    ]
    return lax.ppermute(x, "ctx", pairs)


def routing(expert_ids, gate_weights, experts, capacity):
    rows = expert_ids.shape[0]
    names = jnp.arange(experts, dtype=jnp.int32)
    hit = expert_ids[:, :, None] == names
    member = jnp.any(hit, axis=1)
    gate = jnp.sum(jnp.where(hit, gate_weights[:, :, None], 0.0), axis=1)
    order = jnp.arange(rows, dtype=jnp.int32)
    earlier = (order[:, None] > order[None, :]).astype(jnp.bfloat16)
    slot = jnp.dot(earlier, member.astype(jnp.bfloat16), preferred_element_type=jnp.float32)
    slot = jnp.where(member, slot.astype(jnp.int32), -1)
    slots = jnp.arange(capacity, dtype=jnp.int32)
    taken = slot.T[:, None, :] == slots[None, :, None]
    send = taken.astype(jnp.bfloat16).reshape(experts * capacity, rows)
    taken_back = slot[:, :, None] == slots[None, None, :]
    high = gate.astype(jnp.bfloat16)
    low = (gate - high.astype(jnp.float32)).astype(jnp.bfloat16)
    zero = jnp.zeros((), jnp.bfloat16)
    weigh = lambda g: jnp.where(taken_back, g[:, :, None], zero).reshape(rows, experts * capacity)
    return send, jnp.concatenate([weigh(high), weigh(low)], axis=0)


def dot32(a, b):
    return jnp.dot(a, b, preferred_element_type=jnp.float32)


def whole(a):
    return pl.BlockSpec(a.shape, lambda i: (0,) * a.ndim)


def slab_of(a, n):
    return pl.BlockSpec((a.shape[0], 128, a.shape[2]), lambda i: (0, n, 0))


def one_of(a):
    return pl.BlockSpec((1,) + a.shape[1:], lambda i: (i,) + (0,) * (a.ndim - 1))


def call(kernel, name, grid, inputs, in_specs, outputs, out_specs, flops, scratch=(), aliases={}, limit=VMEM_LIMIT):
    size = lambda a: a.size * a.dtype.itemsize
    return pl.pallas_call(
        kernel,
        grid=(grid,),
        in_specs=in_specs,
        out_specs=out_specs,
        out_shape=outputs,
        scratch_shapes=list(scratch),
        input_output_aliases=aliases,
        compiler_params=pltpu.CompilerParams(vmem_limit_bytes=limit),
        cost_estimate=pl.CostEstimate(
            flops=flops,
            bytes_accessed=sum(size(a) for a in inputs) + sum(size(a) for a in outputs),
            transcendentals=0,
        ),
        name=name,
    )(*inputs)


def out_like(shape, dtype):
    return jax.ShapeDtypeStruct(shape, dtype)


def prepare_kernel(where_ref, tokens_ref, qkv_ref, out_ref, spread_ref, second_ref, normed_ref):
    own_width = second_ref.shape[1]
    width_heads = HEADS * HD
    shard_rows = qkv_ref.shape[0]
    share = out_ref.shape[1] // 2
    at = lambda start, size: pl.ds(pl.multiple_of(start, size), size)
    part = lambda n: qkv_ref[:, at(n * width_heads + where_ref[0] * own_width, own_width)]
    normed_ref[...] = rms_rows(tokens_ref[...].astype(jnp.float32)).astype(jnp.bfloat16)
    keys, values = part(1), part(2)
    for n in range(spread_ref.shape[0]):
        spread_ref[n, :, :own_width] = keys
        spread_ref[n, :, own_width:] = values

    @pl.when(pl.program_id(0) == 0)
    def _():
        second_ref[:shard_rows] = part(0)
        rows = out_ref.shape[0]
        for n in range(share // own_width):
            columns = at((where_ref[0] & 1) * share + n * own_width, own_width)
            second_ref[shard_rows + n * rows : shard_rows + (n + 1) * rows] = out_ref[:, columns]


def prepared(place, tokens, qkv_weight, out_weight, own_width, experts):
    steps = 4
    rows, width = tokens.shape
    stacked = qkv_weight.shape[0] + out_weight.shape[0] * (width // 2 // own_width)
    inputs = [place.reshape(1), tokens, qkv_weight, out_weight]
    outputs = [
        out_like((experts, qkv_weight.shape[0], 2 * own_width), jnp.bfloat16),
        out_like((stacked, own_width), jnp.bfloat16),
        out_like((rows, width), jnp.bfloat16),
    ]
    slab = lambda a: pl.BlockSpec((a.shape[0] // steps,) + a.shape[1:], lambda i: (i,) + (0,) * (a.ndim - 1))
    return call(
        prepare_kernel, "prepared", steps, inputs,
        [pl.BlockSpec(memory_space=pltpu.SMEM), slab(tokens), whole(qkv_weight), whole(out_weight)],
        outputs, [slab(outputs[0]), whole(outputs[1]), slab(outputs[2])], 4 * tokens.size,
        limit=HIGH_VMEM_LIMIT,
    )


def key_value_kernel(w_ref, *refs):
    rows_refs, (pair_ref, sent_ref) = refs[:GROUP], refs[GROUP:]
    own_width = w_ref.shape[1] // 2
    for j, x_ref in enumerate(rows_refs):

        @pl.when(pl.program_id(0) == j)
        def _(x_ref=x_ref):
            both = dot32(x_ref[...], w_ref[...])
            keys = jax.nn.silu(both[:, :own_width]).astype(jnp.bfloat16)
            values = both[:, own_width:].astype(jnp.bfloat16)
            pair_ref[0, :, :own_width] = keys
            pair_ref[0, :, own_width:] = values
            for h in range(own_width // HD):
                cut = slice(h * HD, (h + 1) * HD)
                state = lax.dot_general(
                    keys[:, cut],
                    values[:, cut],
                    (((0,), (0,)), ((), ())),
                    preferred_element_type=jnp.float32,
                )
                sent_ref[0, h] = state.astype(jnp.bfloat16)


def keys_values_states(weight, everyone):
    rows, width = everyone[0].shape
    columns = weight.shape[1]
    heads = columns // 2 // HD
    pair = out_like((GROUP, rows, columns), jnp.bfloat16)
    sent = out_like((GROUP, heads, HD, HD), jnp.bfloat16)
    inputs = [weight, *everyone]
    outputs = [pair, sent]
    flops = 2 * GROUP * rows * width * columns
    return call(
        key_value_kernel, "keys_values_states", GROUP, inputs, [whole(a) for a in inputs],
        outputs, [one_of(a) for a in outputs], flops,
    )


def query_kernel(w_ref, pair_ref, *refs):
    rows_refs, (query_ref, inside_ref) = refs[:GROUP], refs[GROUP:]
    own_width = w_ref.shape[2]
    rows = pair_ref.shape[1]
    for j, x_ref in enumerate(rows_refs):

        @pl.when(pl.program_id(0) == j)
        def _(x_ref=x_ref):
            weight = w_ref[...].reshape(-1, own_width)
            query_ref[0] = jax.nn.silu(dot32(x_ref[...], weight)).astype(jnp.bfloat16)

    causal = lax.broadcasted_iota(jnp.int32, (rows, rows), 0) >= lax.broadcasted_iota(
        jnp.int32, (rows, rows), 1
    )
    for h in range(own_width // HD):
        keys = pair_ref[0, :, h * HD : (h + 1) * HD]
        values = pair_ref[0, :, own_width + h * HD : own_width + (h + 1) * HD]
        scores = lax.dot_general(
            query_ref[0, :, h * HD : (h + 1) * HD],
            keys,
            (((1,), (1,)), ((), ())),
            preferred_element_type=jnp.float32,
        )
        scores = jnp.where(causal, scores, 0.0).astype(jnp.bfloat16)
        inside_ref[0, :, h * HD : (h + 1) * HD] = dot32(scores, values)


def queries_inside(weight, pair, everyone):
    rows, width = everyone[0].shape
    own_width = weight.shape[2]
    inputs = [weight, pair, *everyone]
    outputs = [
        out_like((GROUP, rows, own_width), jnp.bfloat16),
        out_like((GROUP, rows, own_width), jnp.float32),
    ]
    flops = 2 * GROUP * rows * own_width * (width + 2 * rows)
    return call(
        query_kernel, "queries_inside", GROUP, inputs,
        [slab_of(weight, 0), one_of(pair)] + [whole(a) for a in everyone],
        outputs, [one_of(a) for a in outputs], flops,
    )


def finish_kernel(where_ref, query_ref, inside_ref, base_ref, *refs):
    across, out_ref = refs[:-1], refs[-1]
    for h in range(base_ref.shape[1]):
        carried = base_ref[0, h]
        for d, ref in enumerate(across):
            reached = (where_ref[0] > d).astype(jnp.float32)
            carried = carried + ref[0, h].astype(jnp.float32) * reached
        high = carried.astype(jnp.bfloat16)
        low = (carried - high.astype(jnp.float32)).astype(jnp.bfloat16)
        cut = slice(h * HD, (h + 1) * HD)
        query = query_ref[0, :, cut]
        mixed = dot32(query, high) + dot32(query, low) + inside_ref[0, :, cut]
        out_ref[0, :, cut] = rms_rows(mixed).astype(jnp.bfloat16)


def finished_heads(column, query, inside, base, across):
    inputs = [column.reshape(1), query, inside, base, *across]
    specs = [pl.BlockSpec(memory_space=pltpu.SMEM)] + [one_of(a) for a in inputs[1:]]
    output = out_like(query.shape, jnp.bfloat16)
    return call(
        finish_kernel, "finished_heads", GROUP, inputs, specs, [output], [one_of(output)],
        4 * query.size * HD,
    )[0]


def project_kernel(where_ref, tokens_ref, send_ref, *refs):
    back, slabs = refs[:GROUP], refs[GROUP : GROUP + 4]
    hidden_ref, rows_ref, ordered_ref, sum_ref, normed_ref = refs[GROUP + 4 :]
    own_width = back[0].shape[1]
    count, stacked, narrow = slabs[0].shape
    shard = ordered_ref.shape[1] // count
    parts = stacked // shard
    step = pl.program_id(0)

    @pl.when(step == 0)
    def _():
        for j, ref in enumerate(back):
            at = pl.multiple_of((where_ref[0] ^ j) * own_width, own_width)
            ordered_ref[:, pl.ds(at, own_width)] = ref[...]
        heads = ordered_ref[...]
        for j, ref in enumerate(slabs):
            for n in range(parts):
                weight = ref[:, n * shard : (n + 1) * shard, :].reshape(count * shard, narrow)
                at = ((where_ref[0] & 1) ^ (j // 2)) * 2 * parts + j % 2 * parts + n
                at = pl.multiple_of(at * narrow, narrow)
                sum_ref[:, pl.ds(at, narrow)] = dot32(heads, weight)
        hidden = (tokens_ref[...].astype(jnp.float32) + sum_ref[...]).astype(jnp.bfloat16)
        hidden_ref[...] = hidden
        normed_ref[...] = rms_rows(hidden.astype(jnp.float32)).astype(jnp.bfloat16)

    rows_ref[...] = dot32(send_ref[...], normed_ref[...]).astype(jnp.bfloat16)


def projected_rows(place, tokens, send, back, halves):
    rows, width = tokens.shape
    slots = send.shape[0]
    tile = 384
    inputs = [place.reshape(1), tokens, send, *back, halves[0], halves[0], halves[1], halves[1]]
    specs = [pl.BlockSpec(memory_space=pltpu.SMEM), whole(tokens)]
    specs += [pl.BlockSpec((tile, rows), lambda i: (i, 0))]
    specs += [whole(a) for a in back] + [slab_of(a, n) for a in halves for n in (1, 2)]
    outputs = [
        out_like((rows, width), jnp.bfloat16),
        out_like((slots, width), jnp.bfloat16),
    ]
    out_specs = [
        whole(outputs[0]),
        pl.BlockSpec((tile, width), lambda i: (i, 0)),
    ]
    scratch = [
        pltpu.VMEM((rows, GROUP * back[0].shape[1]), jnp.bfloat16),
        pltpu.VMEM((rows, width), jnp.float32),
        pltpu.VMEM((rows, width), jnp.bfloat16),
    ]
    flops = 2 * rows * width * (slots + GROUP * back[0].shape[1])
    return call(
        project_kernel, "projected_rows", slots // tile, inputs, specs, outputs, out_specs, flops, scratch
    )


def expert_kernel(rows_ref, gate_ref, up_ref, out_weight_ref, out_ref, middle_ref):
    step = pl.program_id(0)
    inner = gate_ref.shape[1]
    chunks = FF // inner
    tile = ROW_TILE
    tiles = rows_ref.shape[0] // tile

    @pl.when(step < chunks)
    def _():
        at = pl.multiple_of(step * inner, inner)
        for r in range(tiles):
            cut = slice(r * tile, (r + 1) * tile)
            gate = dot32(rows_ref[cut, :], gate_ref[...])
            up = dot32(rows_ref[cut, :], up_ref[...])
            middle_ref[cut, pl.ds(at, inner)] = (jax.nn.silu(gate) * up).astype(jnp.bfloat16)

    @pl.when(step >= chunks)
    def _():
        for r in range(tiles):
            cut = slice(r * tile, (r + 1) * tile)
            out_ref[cut, :] = dot32(middle_ref[cut, :], out_weight_ref[...]).astype(jnp.bfloat16)


def expert_rows(rows, inner_weight, outer_weight):
    count, width = rows.shape
    chunks, inner, outer = FF // 512, 512, 1024
    last = chunks - 1
    inputs = [rows, inner_weight, inner_weight, outer_weight]
    output = out_like((count, width), jnp.bfloat16)
    specs = [
        whole(rows),
        pl.BlockSpec((width, inner), lambda i: (0, jnp.minimum(i, last))),
        pl.BlockSpec((width, inner), lambda i: (0, chunks + jnp.minimum(i, last))),
        pl.BlockSpec((FF, outer), lambda i: (0, jnp.maximum(i - chunks, 0))),
    ]
    out_spec = pl.BlockSpec((count, outer), lambda i: (0, jnp.maximum(i - chunks, 0)))
    return call(
        expert_kernel, "expert_rows", chunks + width // outer, inputs, specs, [output], [out_spec],
        2 * count * width * 3 * FF, [pltpu.VMEM((count, FF), jnp.bfloat16)],
    )[0]


def shards(
    tokens, qkv_weight, out_weight, prior_state, expert_ids, gate_weights, expert_in, expert_out
):
    rows, width = tokens.shape
    width_heads = HEADS * HD
    experts = lax.axis_size("ctx")
    capacity = 3 * rows * expert_ids.shape[1] // (2 * experts)
    own_heads = HEADS // GROUP
    own_width = own_heads * HD
    place = lax.axis_index("dp") % GROUP
    column = lax.axis_index("ctx") // SIDE
    row = lax.axis_index("ctx") % SIDE
    cut = lambda a, start, size, axis: lax.dynamic_slice_in_dim(a, start, size, axis=axis)

    spread, second, normed = prepared(place, tokens, qkv_weight, out_weight, own_width, experts)
    second = lax.all_gather(second[None], "ctx", axis=0, tiled=True)
    far = swap_with(normed, 2)
    near = swap_with(normed, 1)
    first = lax.all_to_all(spread, "ctx", split_axis=0, concat_axis=0, tiled=True)
    everyone = [normed, near, far, swap_with(far, 1)]
    prior = [cut(prior_state, place * own_heads, own_heads, 0)]
    for other in range(1, GROUP):
        prior.append(swap_with(cut(prior_state, (place ^ other) * own_heads, own_heads, 0), other))
    send, weigh = routing(expert_ids, gate_weights, experts, capacity)
    first, prior, send, weigh = lax.optimization_barrier((first, tuple(prior), send, weigh))
    prior = jnp.stack(prior)

    pair, sent = keys_values_states(first.reshape(width, 2 * own_width), everyone)
    in_row = [shift_ctx(sent, 0, d).astype(jnp.float32) for d in range(1, SIDE)]
    total = (sent.astype(jnp.float32) + in_row[0] + in_row[1] + in_row[2]).astype(jnp.bfloat16)
    base = prior
    for d in range(1, SIDE):
        base = base + jnp.where(row >= d, in_row[d - 1], 0.0)

    second, _ = lax.optimization_barrier((second, total))
    across = [shift_ctx(total, d, 0) for d in range(1, SIDE)]
    query, inside = queries_inside(second, pair, everyone)
    halves = [second, swap_with(second, 1)]

    head_normed = finished_heads(column, query, inside, base, across)
    back = [head_normed[0]] + [swap_with(head_normed[j], j) for j in range(1, GROUP)]
    hidden, outgoing = projected_rows(place, tokens, send, back, halves)

    outgoing, weigh, hidden = lax.optimization_barrier((outgoing, weigh, hidden))
    outgoing = outgoing.reshape(experts, capacity, width)
    arrived = lax.all_to_all(outgoing, "ctx", split_axis=0, concat_axis=0, tiled=True)
    grouped = arrived.reshape(experts * capacity, width)
    result = expert_rows(grouped, expert_in[0], expert_out[0])
    result, weigh, hidden = lax.optimization_barrier((result, weigh, hidden))
    returned = lax.all_to_all(
        result.reshape(experts, capacity, width), "ctx", split_axis=0, concat_axis=0, tiled=True
    ).reshape(experts * capacity, width)
    combined = jnp.dot(weigh, returned, preferred_element_type=jnp.float32)
    return (hidden.astype(jnp.float32) + (combined[:rows] + combined[rows:])).astype(jnp.bfloat16)


def solution(mesh):
    return jax.shard_map(
        shards,
        mesh=mesh,
        in_specs=(
            P(("dp", "ctx"), None),
            P("ctx", None),
            P("ctx", None),
            P("dp", None, None),
            P(("dp", "ctx"), None),
            P(("dp", "ctx"), None),
            P("ctx", None, None),
            P("ctx", None, None),
        ),
        out_specs=P(("dp", "ctx"), None),
        check_vma=False,
    )
```
